512 devices in a mesh: sweep: 32 (over x, z_hi, core), span: 16 (over z_lo, y).
Axes of the slice: x: 4, y: 8, z: 8 (z_hi: 4, z_lo: 2; z = z_hi * 2 + z_lo), core: 2. Of those that a mesh axis runs over, the one named last changes fastest.
Arguments:
- inverses: bfloat16 [32, 16, 6, 135, 135], P('sweep', 'span')
- couplings: bfloat16 [6, 32, 16, 6, 135, 135], P(None, 'sweep', 'span')
- rhs: bfloat16 [32, 16, 6, 135, 128], P('sweep', 'span'), may hold values from -6 to 6
- previous: bfloat16 [32, 16, 6, 135, 128], P('sweep', 'span'), may hold values from -6 to 6
- slot_layer: int32 [32, 16, 6], P('sweep', 'span'), may hold values from 0 to 5, each once within a row
Outputs:
- solution: float32 [32, 16, 6, 135, 128], P('sweep', 'span')
The draws below stay inside these ranges and needn't reach their ends.
Inputs may be any that keep to these rules, and one draw needn't show every extreme that they name: `slot_layer`: in each line each wall-normal layer is stored in exactly one slot.
All inputs are finite; a program needn't handle non-finite values.
Results may differ from the reference program's by a relative error of at most 0.0029.
Values may be sent and summed in bfloat16 or wider, within the bound.
No kernel may reach another device: no remote copies, remote signals or barrier semaphores. Data moves between devices by JAX's collectives and lax.ppermute only.
A program may use at most 128 MiB of HBM per device.

```python
import math
import jax
import jax.numpy as jnp
from jax import lax

BS = 135
NRHS = 128
NZ = 6
NX = 32
NY = 16


def draw_inverses(key, part):
    shape = (NX, NY, NZ, BS, BS)
    noise = jax.random.normal(key, shape, jnp.float32)
    unit = jnp.eye(BS, dtype=jnp.float32)
    return (0.5 * (unit + 0.5 * noise / math.sqrt(BS))).astype(jnp.bfloat16)


def draw_couplings(key, part):
    shape = (6, NX, NY, NZ, BS, BS)
    noise = jnp.clip(jax.random.normal(key, shape, jnp.float32), -4.0, 4.0)
    face_scale = jnp.array([1.7, 1.0, 1.0, 1.0, 1.0, 1.0], jnp.float32).reshape(6, 1, 1, 1, 1, 1)
    return (noise * face_scale / math.sqrt(BS)).astype(jnp.bfloat16)


def block_scale(rng, extent, shards, least, top_value):
    level, own = 1.0, jax.random.fold_in(rng, 6)
    for dim, blocks in shards:
        draws = jnp.exp(jax.random.uniform(jax.random.fold_in(own, dim), (blocks,), jnp.float32, least / len(shards), top_value / len(shards)))
        level = level * jnp.repeat(draws, extent[dim] // blocks).reshape([-1 if axis == dim else 1 for axis in range(len(extent))])
    return level


def centred(own_key, shape, spread, most, split=(), kind=jnp.bfloat16):
    values = jax.random.normal(own_key, shape, jnp.float32) * spread
    if len(split) > 0:
        values = block_scale(own_key, shape, split, -0.22, 0.18) * values
    return jnp.clip(values, min=-most, max=most).astype(kind)


def setup_inputs(seed: int = 0) -> dict:
    streams_of = jax.random.split(jax.random.key(seed), 6)
    return {
        "inverses": draw_inverses(jax.random.fold_in(streams_of[5], 71), 0),
        "couplings": draw_couplings(jax.random.fold_in(streams_of[5], 71), 0),
        "rhs": centred(streams_of[2], (NX, NY, NZ, BS, NRHS), 1.0, 6.0, ((0, 32), (1, 16))),
        "previous": centred(streams_of[3], (NX, NY, NZ, BS, NRHS), 1.0, 6.0, ((0, 32), (1, 16))),
        "slot_layer": jax.vmap(lambda own: jax.random.permutation(own, NZ))(jax.random.split(streams_of[4], NX * NY)).reshape((NX, NY, NZ)).astype(jnp.int32),
    }


def couple(blocks, vectors):
    return jnp.einsum("...ab,...br->...ar", blocks.astype(jnp.float32), vectors.astype(jnp.float32), precision=lax.Precision.HIGHEST)


def select_layers(slot_layer, values, step_by):
    chooser = (slot_layer[:, :, None, :] == slot_layer[:, :, :, None] + step_by).astype(jnp.float32)
    picked = jnp.einsum("ijst,ijtbr->ijsbr", chooser, values.astype(jnp.float32), precision=lax.Precision.HIGHEST)
    return picked.astype(jnp.bfloat16)


def reference(inverses, couplings, rhs, previous, slot_layer):
    downstream = jnp.concatenate([previous[1:], jnp.zeros_like(previous[:1])], axis=0)
    span_lower = jnp.roll(previous, 1, axis=1)
    span_upper = jnp.roll(previous, -1, axis=1)
    wall_lower = select_layers(slot_layer, previous, -1)
    wall_upper = select_layers(slot_layer, previous, 1)
    coupled = couple(couplings[1], downstream)
    coupled = coupled + couple(couplings[2], span_lower)
    coupled = coupled + couple(couplings[3], span_upper)
    coupled = coupled + couple(couplings[4], wall_lower)
    coupled = coupled + couple(couplings[5], wall_upper)
    forcing = (rhs.astype(jnp.float32) - coupled).astype(jnp.bfloat16)
    offset = couple(inverses, forcing)
    transfer = -couple(inverses, couplings[0])

    def advance(inflow, pieces):
        matrix, shift_term = pieces
        fresh = shift_term + jnp.einsum("lzab,lzbr->lzar", matrix, inflow, precision=lax.Precision.HIGHEST)
        return fresh, fresh

    initial = jnp.zeros(offset.shape[1:], jnp.float32)
    unused, solution = lax.scan(advance, initial, (transfer, offset))
    return solution
```

```python
import jax
import jax.numpy as jnp
from jax import lax
from jax.experimental import pallas as pl
from jax.experimental.pallas import tpu as pltpu
from jax.sharding import PartitionSpec as P

BS, NRHS, NZ = 135, 128, 6
ROWS = 136
LANE = 128
HALF = NZ // 2
NX_CHIPS, NZ_CHIPS = 4, 4
F32, BF16 = jnp.float32, jnp.bfloat16

SMEM = pl.BlockSpec(memory_space=pltpu.SMEM)
VMEM = pl.BlockSpec(memory_space=pltpu.VMEM)


def sweep_index(x, z, core):
    return (x * NZ_CHIPS + z) * 2 + core


Z_GROUPS = [[sweep_index(x, z, c) for z in range(NZ_CHIPS)] for x in range(NX_CHIPS) for c in range(2)]
X_GROUPS = [[sweep_index(x, z, c) for x in range(NX_CHIPS)] for z in range(NZ_CHIPS) for c in range(2)]


def face(index):
    return pl.BlockSpec((1, 1, 1, NZ, BS, BS), lambda i: (index, 0, 0, 0, 0, 0))


def mm(a, b):
    return jnp.dot(a, b, preferred_element_type=F32)


def split(v):
    hi = v.astype(BF16)
    return hi, (v - hi.astype(F32)).astype(BF16)


def mm3(a, b):
    return mm(a[0], b[0]) + (mm(a[0], b[1]) + mm(a[1], b[0]))


def pack(ref, at, main, tail, shift):
    r = main.shape[0]
    for place, value in ((0, main), (3, shift)):
        hi, lo = split(value)
        ref[at + (place, slice(0, r))] = hi
        ref[at + (place + 1, slice(0, r))] = lo
    hi, lo = split(tail)
    both = hi.astype(F32) + pltpu.roll(lo.astype(F32), 8, 1)
    ref[at + (2, slice(0, r))] = both.astype(BF16)


def unpack_tail(block):
    both = block.astype(F32)
    lane = lax.broadcasted_iota(jnp.int32, both.shape, 1)
    hi = jnp.where(lane < 8, both, 0.0)
    lo = jnp.where(lane < 8, pltpu.roll(both, LANE - 8, 1), 0.0)
    return hi, lo


def load_matrix(ref, at, scratch):
    tails = unpack_tail(ref[at + (2,)])
    for k in range(2):
        scratch[k, :, :LANE] = ref[at + (k,)]
        scratch[k, :, LANE:] = tails[k].astype(BF16)
    return scratch[0, :BS, :BS], scratch[1, :BS, :BS]


def load_shift(ref, at):
    return ref[at + (3, slice(0, BS))].astype(F32) + ref[at + (4, slice(0, BS))].astype(F32)


def transfer_kernel(inv, c0, out):
    for s in range(NZ):
        out[s] = -mm(inv[s], c0[0, 0, 0, s])


def wall_kernel(layers, c4, c5, rhs, prev, out):
    for s in range(NZ):
        layer = layers[s]
        total = rhs[s].astype(F32)
        for step, blocks in ((-1, c4), (1, c5)):
            found, exists = 0, 0
            for t in range(NZ):
                match = layers[t] == layer + step
                found = jnp.where(match, t, found)
                exists = jnp.where(match, 1, exists)
            keep = jnp.full((BS, NRHS), exists, jnp.int32) > 0
            vectors = jnp.where(keep, prev[found].astype(F32), 0.0).astype(BF16)
            total = total - mm(blocks[0, 0, 0, s], vectors)
        out[s] = total


def pair_kernel(core, own, sib, packed, second_out, final_out, scratch):
    c = core[0]
    scratch[...] = jnp.zeros_like(scratch)

    def body(first, second, mine):
        for s in range(NZ):
            t1 = split(second[s])
            second_out[s, 0], second_out[s, 1] = t1
            if mine == 0:
                final_out[s, 0], final_out[s, 1] = split(first[s])
                if s >= HALF:
                    continue
            a = mm3(t1, split(first[s]))
            if mine == 1:
                final_out[s, 0], final_out[s, 1] = split(a)
            if s // HALF == mine:
                scratch[:BS, :BS] = a
                for place, value in ((0, scratch[:, :LANE]),):
                    hi, lo = split(value)
                    packed[s % HALF, place] = hi
                    packed[s % HALF, place + 1] = lo
                hi, lo = split(scratch[:, LANE:])
                packed[s % HALF, 2] = (hi.astype(F32) + pltpu.roll(lo.astype(F32), 8, 1)).astype(BF16)

    pl.when(c == 0)(lambda: body(own, sib, 0))
    pl.when(c == 1)(lambda: body(sib, own, 1))


def offset_kernel(inv, c1, c2, c3, partial, down, lower, upper, out):
    for s in range(NZ):
        total = mm(c1[0, 0, 0, s], down[s]) + mm(c2[0, 0, 0, s], lower[s]) + mm(c3[0, 0, 0, s], upper[s])
        forcing = (partial[s] - total).astype(BF16)
        out[s] = mm(inv[s], forcing)


def send_kernel(core, second, own, sib, packed, send, shift_out):
    c = core[0]
    for s in range(HALF):
        send[s, 0:3] = packed[s]
    send[HALF] = jnp.zeros_like(send[HALF])

    def body(first_o, second_o, mine):
        for s in range(NZ):
            if mine == 0:
                shift_out[s] = first_o[s]
                if s >= HALF:
                    continue
            b = mm3((second[s, 0], second[s, 1]), split(first_o[s])) + second_o[s]
            if mine == 1:
                shift_out[s] = b
            if s // HALF == mine:
                send[s % HALF, 3, :BS], send[s % HALF, 4, :BS] = split(b)

    pl.when(c == 0)(lambda: body(own, sib, 0))
    pl.when(c == 1)(lambda: body(sib, own, 1))


def chain_kernel(recv, prefix, total, mat):
    tail = unpack_tail(recv[0, 2])
    main = recv[0, 0].astype(F32) + recv[0, 1].astype(F32)
    state = jnp.concatenate([main[:BS], load_shift(recv, (0,)), (tail[0] + tail[1])[:BS]], axis=1)
    for k in range(1, NZ_CHIPS + 1):
        if k > 1:
            fresh = mm3(load_matrix(recv, (k - 1,), mat), split(state))
            state = jnp.concatenate(
                [fresh[:, :LANE], fresh[:, LANE : 2 * LANE] + load_shift(recv, (k - 1,)), fresh[:, 2 * LANE :]], axis=1
            )
        parts = state[:, :LANE], state[:, 2 * LANE :], state[:, LANE : 2 * LANE]
        if k < NZ_CHIPS:
            pack(prefix, (k - 1,), *parts)
        else:
            for x in range(NX_CHIPS):
                pack(total, (x,), *parts)


def state_kernel(place, totals, prefix, send, state, mat):
    x = place[0]
    first = jnp.full((BS, NRHS), x, jnp.int32) > 0
    state[...] = jnp.where(first, load_shift(totals, (0,)), 0.0)
    for g in range(1, NX_CHIPS - 1):

        @pl.when(x > g)
        def _(g=g):
            state[...] = mm3(load_matrix(totals, (g,), mat), split(state[...])) + load_shift(totals, (g,))

    inflow = split(state[...])
    send[0, :BS] = inflow[0]
    for k in range(1, NZ_CHIPS):
        send[k, :BS] = (mm3(load_matrix(prefix, (k - 1,), mat), inflow) + load_shift(prefix, (k - 1,))).astype(BF16)


def final_kernel(core, matrix, shift, own, sib, out):
    c = core[0]

    def body(mine):
        for s in range(NZ):
            source = own if s // HALF == mine else sib
            v = source[s % HALF, :BS]
            out[s] = shift[s] + (mm(matrix[s, 0], v) + mm(matrix[s, 1], v))

    pl.when(c == 0)(lambda: body(0))
    pl.when(c == 1)(lambda: body(1))


def shape(*dims, dtype=F32):
    return jax.ShapeDtypeStruct(dims, dtype)


def call(kernel, outs, specs, scratch=(), **kw):
    single = not isinstance(outs, tuple)
    return pl.pallas_call(
        kernel,
        grid=(1,),
        out_shape=outs,
        in_specs=specs,
        out_specs=VMEM if single else (VMEM,) * len(outs),
        scratch_shapes=scratch,
        name=kernel.__name__,
        **kw,
    )


def local(inverses, couplings, rhs, previous, slot_layer):
    inv, rhs, prev, layers = inverses[0, 0], rhs[0, 0], previous[0, 0], slot_layer[0, 0]
    place = lax.axis_index("sweep")
    core = (place % 2).reshape(1).astype(jnp.int32)
    group = (place // (2 * NZ_CHIPS)).reshape(1).astype(jnp.int32)
    n_sweep, n_span = lax.axis_size("sweep"), lax.axis_size("span")
    swap = [(i, i ^ 1) for i in range(n_sweep)]

    lower = lax.ppermute(prev, "span", [(i, (i + 1) % n_span) for i in range(n_span)])
    upper = lax.ppermute(prev, "span", [((i + 1) % n_span, i) for i in range(n_span)])
    down = lax.ppermute(prev, "sweep", [(i + 1, i) for i in range(n_sweep - 1)])

    t_own = call(transfer_kernel, shape(NZ, BS, BS), [VMEM, face(0)])(inv, couplings)
    t_sib = lax.ppermute(t_own, "sweep", swap)
    partial = call(wall_kernel, shape(NZ, BS, NRHS), [SMEM, face(4), face(5), VMEM, VMEM])(layers, couplings, couplings, rhs, prev)
    packed, second, matrix = call(
        pair_kernel,
        (shape(HALF, 3, ROWS, LANE, dtype=BF16), shape(NZ, 2, BS, BS, dtype=BF16), shape(NZ, 2, BS, BS, dtype=BF16)),
        [SMEM, VMEM, VMEM],
        [pltpu.VMEM((ROWS, 2 * LANE), F32)],
    )(core, t_own, t_sib)
    o_own = call(offset_kernel, shape(NZ, BS, NRHS), [VMEM, face(1), face(2), face(3)] + [VMEM] * 4)(
        inv, couplings, couplings, couplings, partial, down, lower, upper
    )
    o_sib = lax.ppermute(o_own, "sweep", swap)
    send, shift = call(
        send_kernel, (shape(NZ_CHIPS, 5, ROWS, LANE, dtype=BF16), shape(NZ, BS, NRHS)), [SMEM] + [VMEM] * 4
    )(core, second, o_own, o_sib, packed)
    recv = lax.all_to_all(send, "sweep", 0, 0, axis_index_groups=Z_GROUPS)
    mat = pltpu.VMEM((2, ROWS, 2 * LANE), BF16)
    prefix, total = call(
        chain_kernel,
        (shape(NZ_CHIPS - 1, 5, ROWS, LANE, dtype=BF16), shape(NX_CHIPS, 5, ROWS, LANE, dtype=BF16)),
        [VMEM],
        [mat],
    )(recv)
    totals = lax.all_to_all(total, "sweep", 0, 0, axis_index_groups=X_GROUPS)
    back = call(
        state_kernel,
        shape(NZ_CHIPS, ROWS, NRHS, dtype=BF16),
        [SMEM, VMEM, VMEM],
        [pltpu.VMEM((BS, NRHS), F32), mat],
    )(group, totals, prefix)
    mine = lax.all_to_all(back, "sweep", 0, 0, axis_index_groups=Z_GROUPS)
    theirs = lax.ppermute(mine, "sweep", swap)
    out = call(final_kernel, shape(NZ, BS, NRHS), [SMEM] + [VMEM] * 4)(core, matrix, shift, mine, theirs)
    return out[None, None]


def solution(mesh):
    return jax.shard_map(
        local,
        mesh=mesh,
        in_specs=(
            P("sweep", "span", None, None, None),
            P(None, "sweep", "span", None, None, None),
            P("sweep", "span", None, None, None),
            P("sweep", "span", None, None, None),
            P("sweep", "span", None),
        ),
        out_specs=P("sweep", "span", None, None, None),
        check_vma=False,
    )
```

```python
import jax
import jax.numpy as jnp
from jax import lax
from jax.experimental import pallas as pl
from jax.experimental.pallas import tpu as pltpu
from jax.sharding import PartitionSpec as P


BS, NRHS, NZ = 135, 128, 6
LANE = 128
HALF = NZ // 2
RUN = 4
GROUPS = 4
ROWS = 136
SECOND, TAILS, FOLD = 144, 288, 24
PACKED = TAILS + FOLD
F32, BF16 = jnp.float32, jnp.bfloat16

RUNS = [[(g * RUN + m) * 2 + c for m in range(RUN)] for g in range(GROUPS) for c in range(2)]
ACROSS = [[(g * RUN + m) * 2 + c for g in range(GROUPS)] for m in range(RUN) for c in range(2)]
SHIFT = PACKED + 8
LOW = SHIFT + SECOND
AFFINE = LOW + SECOND


def mm(a, b):
    return jnp.dot(a, b, preferred_element_type=F32)


def split(v):
    hi = v.astype(BF16)
    return hi, (v - hi.astype(F32)).astype(BF16)


def mm3(a, b):
    return mm(a[0], b[0]) + (mm(a[0], b[1]) + mm(a[1], b[0]))


def pack(ref, at, pair, scratch):
    for k in range(2):
        ref[at + (slice(k * SECOND, k * SECOND + BS),)] = pair[k][:, :LANE].astype(BF16)
        scratch[k, :BS, :BS] = pair[k].astype(F32)
    both = scratch[0, :, LANE:] + pltpu.roll(scratch[1, :, LANE:], 8, 1)
    fold = both[:FOLD]
    for g in range(1, SECOND // FOLD):
        fold = fold + pltpu.roll(both[g * FOLD : (g + 1) * FOLD], 16 * g, 1)
    ref[at + (slice(TAILS, PACKED),)] = fold.astype(BF16)


def unpack(ref, at, scratch):
    fold = ref[at + (slice(TAILS, PACKED),)].astype(F32)
    lane = lax.broadcasted_iota(jnp.int32, fold.shape, 1)
    for g in range(SECOND // FOLD):
        rows = slice(g * FOLD, (g + 1) * FOLD)
        for k in range(2):
            shift = (2 * LANE - 16 * g - 8 * k) % LANE
            part = pltpu.roll(fold, shift, 1) if shift else fold
            scratch[k, rows, LANE:] = jnp.where(lane < 8, part, 0.0).astype(BF16)
    for k in range(2):
        scratch[k, :BS, :LANE] = ref[at + (slice(k * SECOND, k * SECOND + BS),)]
    return scratch[0, :BS, :BS], scratch[1, :BS, :BS]


def pack_shift(ref, at, value):
    ref[at + (slice(SHIFT, SHIFT + BS),)], ref[at + (slice(LOW, LOW + BS),)] = split(value)


def unpack_shift(ref, at):
    return ref[at + (slice(SHIFT, SHIFT + BS),)].astype(F32) + ref[at + (slice(LOW, LOW + BS),)].astype(F32)


def transfer_kernel(inv, c0, out):
    for s in range(NZ):
        out[s] = -mm(inv[s], c0[s])


def wall_kernel(layers, c, rhs, prev, out):
    for s in range(NZ):
        layer = layers[s]
        total = rhs[s].astype(F32)
        for step, index in ((-1, 0), (1, 1)):
            found, exists = 0, 0
            for t in range(NZ):
                match = layers[t] == layer + step
                found = jnp.where(match, t, found)
                exists = jnp.where(match, 1, exists)
            keep = jnp.full((BS, NRHS), exists, jnp.int32) > 0
            vectors = jnp.where(keep, prev[found].astype(F32), 0.0).astype(BF16)
            total = total - mm(c[index, s], vectors)
        out[s] = total


def offset_kernel(inv, c, partial, down, lower, upper, out):
    for s in range(NZ):
        total = mm(c[0, s], down[s]) + mm(c[1, s], lower[s]) + mm(c[2, s], upper[s])
        forcing = (partial[s] - total).astype(BF16)
        out[s] = mm(inv[s], forcing)


def pair_kernel(core, own, sib, packed, second_out, final_out, wide):
    c = core[0]
    wide[...] = jnp.zeros_like(wide)

    def body(first, second, mine):
        for s in range(NZ):
            t0, t1 = split(first[s]), split(second[s])
            second_out[s, 0], second_out[s, 1] = t1
            if mine == 0:
                final_out[s, 0], final_out[s, 1] = t0
                if s >= HALF:
                    continue
            both = split(mm3(t1, t0))
            if mine == 1:
                final_out[s, 0], final_out[s, 1] = both
            if s // HALF == mine:
                pack(packed, (s % HALF,), both, wide)

    pl.when(c == 0)(lambda: body(own, sib, 0))
    pl.when(c == 1)(lambda: body(sib, own, 1))


def send_kernel(core, second, own, sib, packed, send, shift_out):
    c = core[0]
    for s in range(HALF):
        send[s, :PACKED] = packed[s]
    send[HALF] = jnp.zeros_like(send[HALF])

    def body(first_o, second_o, mine):
        for s in range(NZ):
            if mine == 0:
                shift_out[s] = first_o[s]
                if s >= HALF:
                    continue
            b = mm3((second[s, 0], second[s, 1]), split(first_o[s])) + second_o[s]
            if mine == 1:
                shift_out[s] = b
            if s // HALF == mine:
                pack_shift(send, (s % HALF,), b)

    pl.when(c == 0)(lambda: body(own, sib, 0))
    pl.when(c == 1)(lambda: body(sib, own, 1))


def chain_kernel(recv, prefix, shifts, total, mat, wide):
    wide[...] = jnp.zeros_like(wide)
    product, state = None, None
    for k in range(RUN):
        a = unpack(recv, (k,), mat.at[k])
        b = unpack_shift(recv, (k,))
        if k == 0:
            product, state = a, b
        else:
            product, state = split(mm3(a, product)), mm3(a, split(state)) + b
        if k < RUN - 1:
            prefix[k, 0], prefix[k, 1] = product
            shifts[k] = state
    for g in range(GROUPS):
        pack(total, (g,), product, wide)
        pack_shift(total, (g,), state)


def state_kernel(place, totals, prefix, shifts, send, state, mat):
    x = place[0]
    first = jnp.full((BS, NRHS), x, jnp.int32) > 0
    state[...] = jnp.where(first, unpack_shift(totals, (0,)), 0.0)
    for g in range(1, GROUPS - 1):

        @pl.when(x > g)
        def _(g=g):
            state[...] = mm3(unpack(totals, (g,), mat), split(state[...])) + unpack_shift(totals, (g,))

    inflow = split(state[...])
    send[0, :BS] = inflow[0]
    for k in range(1, RUN):
        send[k, :BS] = (mm3((prefix[k - 1, 0], prefix[k - 1, 1]), inflow) + shifts[k - 1]).astype(BF16)


def final_kernel(core, matrix, shift, own, sib, out):
    c = core[0]

    def body(mine):
        for s in range(NZ):
            source = own if s // HALF == mine else sib
            v = source[s % HALF, :BS]
            out[s * BS : (s + 1) * BS] = shift[s] + (mm(matrix[s, 0], v) + mm(matrix[s, 1], v))

    pl.when(c == 0)(lambda: body(0))
    pl.when(c == 1)(lambda: body(1))


VMEM = pl.BlockSpec(memory_space=pltpu.VMEM)
SMEM = pl.BlockSpec(memory_space=pltpu.SMEM)
PARAMS = pltpu.CompilerParams(vmem_limit_bytes=20 << 20)


def hbm(*dims, dtype=F32):
    return jax.ShapeDtypeStruct(dims, dtype)


def vmem(*dims, dtype=F32):
    return pltpu.VMEM(dims, dtype)


def call(kernel, outs, args, scratch=()):
    scalar = [a.dtype == jnp.int32 for a in args]
    args = [a if one else pltpu.with_memory_space_constraint(a, pltpu.VMEM) for a, one in zip(args, scalar)]
    return pl.pallas_call(
        kernel,
        out_shape=outs,
        in_specs=[SMEM if one else VMEM for one in scalar],
        out_specs=jax.tree.map(lambda _: VMEM, outs, is_leaf=lambda o: not isinstance(o, tuple)),
        scratch_shapes=scratch,
        name=kernel.__name__,
        compiler_params=PARAMS,
    )(*args)


def local(inverses, couplings, rhs, previous, slot_layer):
    inv, rhs, prev, layers = inverses[0, 0], rhs[0, 0], previous[0, 0], slot_layer[0, 0]
    faces = couplings[:, 0, 0]
    place = lax.axis_index("sweep")
    core = (place % 2).reshape(1).astype(jnp.int32)
    group = (place // (2 * RUN)).reshape(1).astype(jnp.int32)
    n_sweep, n_span = lax.axis_size("sweep"), lax.axis_size("span")
    swap = [(i, i ^ 1) for i in range(n_sweep)]
    wide = pltpu.VMEM((2, SECOND, 2 * LANE), F32)

    lower = lax.ppermute(prev, "span", [(i, (i + 1) % n_span) for i in range(n_span)])
    upper = lax.ppermute(prev, "span", [((i + 1) % n_span, i) for i in range(n_span)])
    down = lax.ppermute(prev, "sweep", [(i + 1, i) for i in range(n_sweep - 1)])

    t_own = call(transfer_kernel, hbm(NZ, BS, BS), [inv, faces[0]])
    t_sib = lax.ppermute(t_own, "sweep", swap)
    partial = call(wall_kernel, vmem(NZ, BS, NRHS), [layers, faces[4:6], rhs, prev])
    packed, second, matrix = call(
        pair_kernel,
        (
            vmem(HALF, PACKED, LANE, dtype=BF16),
            vmem(NZ, 2, BS, BS, dtype=BF16),
            hbm(NZ, 2, BS, BS, dtype=BF16),
        ),
        [core, t_own, t_sib],
        [wide],
    )
    o_own = call(offset_kernel, hbm(NZ, BS, NRHS), [inv, faces[1:4], partial, down, lower, upper])
    o_sib = lax.ppermute(o_own, "sweep", swap)
    send, shift = call(
        send_kernel,
        (hbm(RUN, AFFINE, LANE, dtype=BF16), hbm(NZ, BS, NRHS)),
        [core, second, o_own, o_sib, packed],
    )
    maps = lax.all_to_all(send, "sweep", 0, 0, axis_index_groups=RUNS)
    prefix, shifts, total = call(
        chain_kernel,
        (
            vmem(RUN - 1, 2, BS, BS, dtype=BF16),
            vmem(RUN - 1, BS, NRHS),
            hbm(GROUPS, AFFINE, LANE, dtype=BF16),
        ),
        [maps],
        [pltpu.VMEM((RUN, 2, SECOND, 2 * LANE), BF16), wide],
    )
    totals = lax.all_to_all(total, "sweep", 0, 0, axis_index_groups=ACROSS)
    back = call(
        state_kernel,
        hbm(RUN, ROWS, NRHS, dtype=BF16),
        [group, totals, prefix, shifts],
        [pltpu.VMEM((BS, NRHS), F32), pltpu.VMEM((2, SECOND, 2 * LANE), BF16)],
    )
    mine = lax.all_to_all(back, "sweep", 0, 0, axis_index_groups=RUNS)
    theirs = lax.ppermute(mine, "sweep", swap)
    out = call(final_kernel, hbm(NZ * BS, NRHS), [core, matrix, shift, mine, theirs])
    return out.reshape(1, 1, NZ, BS, NRHS)


def solution(mesh):
    return jax.shard_map(
        local,
        mesh=mesh,
        in_specs=(
            P("sweep", "span", None, None, None),
            P(None, "sweep", "span", None, None, None),
            P("sweep", "span", None, None, None),
            P("sweep", "span", None, None, None),
            P("sweep", "span", None),
        ),
        out_specs=P("sweep", "span", None, None, None),
        check_vma=False,
    )
```

```python
import jax
import jax.numpy as jnp
from jax import lax
from jax.experimental import pallas as pl
from jax.experimental.pallas import tpu as pltpu
from jax.sharding import PartitionSpec as P


BS, NRHS, NZ = 135, 128, 6
LANE = 128
HALF = NZ // 2
RUN = 4
GROUPS = 4
ROWS = 136
SECOND, TAILS, FOLD = 144, 288, 24
PACKED = TAILS + FOLD
F32, BF16 = jnp.float32, jnp.bfloat16

RUNS = [[(g * RUN + m) * 2 + c for m in range(RUN)] for g in range(GROUPS) for c in range(2)]
ACROSS = [[(g * RUN + m) * 2 + c for g in range(GROUPS)] for m in range(RUN) for c in range(2)]
SHIFT = PACKED + 8
LOW = SHIFT + SECOND
CHIP = SHIFT + ROWS
AFFINE = LOW + ROWS


def mm(a, b):
    return jnp.dot(a, b, preferred_element_type=F32)


def split(v):
    hi = v.astype(BF16)
    return hi, (v - hi.astype(F32)).astype(BF16)


def mm3(a, b):
    return mm(a[0], b[0]) + (mm(a[0], b[1]) + mm(a[1], b[0]))


def pack(ref, at, pair, scratch):
    for k in range(2):
        ref[at + (slice(k * SECOND, k * SECOND + BS),)] = pair[k][:, :LANE].astype(BF16)
        scratch[k, :BS, :BS] = pair[k].astype(F32)
    both = scratch[0, :, LANE:] + pltpu.roll(scratch[1, :, LANE:], 8, 1)
    fold = both[:FOLD]
    for g in range(1, SECOND // FOLD):
        fold = fold + pltpu.roll(both[g * FOLD : (g + 1) * FOLD], 16 * g, 1)
    ref[at + (slice(TAILS, PACKED),)] = fold.astype(BF16)


def unpack(ref, at, scratch):
    fold = ref[at + (slice(TAILS, PACKED),)].astype(F32)
    lane = lax.broadcasted_iota(jnp.int32, fold.shape, 1)
    for g in range(SECOND // FOLD):
        rows = slice(g * FOLD, (g + 1) * FOLD)
        for k in range(2):
            shift = (2 * LANE - 16 * g - 8 * k) % LANE
            part = pltpu.roll(fold, shift, 1) if shift else fold
            scratch[k, rows, LANE:] = jnp.where(lane < 8, part, 0.0).astype(BF16)
    for k in range(2):
        scratch[k, :BS, :LANE] = ref[at + (slice(k * SECOND, k * SECOND + BS),)]
    return scratch[0, :BS, :BS], scratch[1, :BS, :BS]


def pack_shift(ref, at, value):
    ref[at + (slice(SHIFT, SHIFT + BS),)], ref[at + (slice(LOW, LOW + BS),)] = split(value)


def unpack_shift(ref, at):
    return ref[at + (slice(SHIFT, SHIFT + BS),)].astype(F32) + ref[at + (slice(LOW, LOW + BS),)].astype(F32)


def local_kernel(core, layers_in, inv_in, c_in, rhs_in, prev_in, inv, c1, transfer, send, partial, layers, c0, walls, rhs, prev, sems):
    moves = (
        (inv_in, inv),
        (c_in.at[0, 0, 0], c0),
        (prev_in, prev),
        (rhs_in, rhs),
        (layers_in, layers),
        (c_in.at[4, 0, 0], walls.at[0]),
        (c_in.at[5, 0, 0], walls.at[1]),
        (c_in.at[1, 0, 0], c1),
    )
    copies = [pltpu.make_async_copy(source, target, sems.at[i]) for i, (source, target) in enumerate(moves)]
    for copy in copies:
        copy.start()
    for copy in copies[:2]:
        copy.wait()
    for s in range(NZ):
        transfer[s, :BS, :BS] = -mm(inv[s], c0[s])
    other = HALF * (1 - core[0])
    for j in range(HALF):
        send[j] = transfer[other + j]
    for copy in copies[2:7]:
        copy.wait()
    for s in range(NZ):
        layer = layers[0, 0, s]
        total = rhs[s].astype(F32)
        for step, index in ((-1, 0), (1, 1)):
            found, exists = 0, 0
            for t in range(NZ):
                match = layers[0, 0, t] == layer + step
                found = jnp.where(match, t, found)
                exists = jnp.where(match, 1, exists)
            keep = jnp.full((BS, NRHS), exists, jnp.int32) > 0
            vectors = jnp.where(keep, prev[found].astype(F32), 0.0).astype(BF16)
            total = total - mm(walls[index, s], vectors)
        partial[s] = total
    for copy in copies[7:]:
        copy.wait()


def product_kernel(core, transfer, sib, packed, wide):
    c = core[0]
    wide[...] = jnp.zeros_like(wide)

    def body(mine):
        for j in range(HALF):
            own, got = split(transfer[mine * HALF + j, :BS, :BS]), split(sib[j, :BS, :BS])
            pack(packed, (j,), split(mm3(got, own) if mine == 0 else mm3(own, got)), wide)

    pl.when(c == 0)(lambda: body(0))
    pl.when(c == 1)(lambda: body(1))


def span_kernel(c_in, partial, lower, upper, out, c, sems):
    copies = [pltpu.make_async_copy(c_in.at[2 + i, 0, 0], c.at[i], sems.at[i]) for i in range(2)]
    for copy in copies:
        copy.start()
    for copy in copies:
        copy.wait()
    for s in range(NZ):
        out[s] = partial[s] - (mm(c[0, s], lower[s]) + mm(c[1, s], upper[s]))


def offset_kernel(core, inv, c1, partial, down, out, send):
    for s in range(NZ):
        forcing = (partial[s] - mm(c1[s], down[s])).astype(BF16)
        out[s] = mm(inv[s], forcing)
    other = HALF * (1 - core[0])
    for j in range(HALF):
        send[j, :BS] = out[other + j]


def pair_kernel(core, packed, transfer, sib, offset, offset_sib, send):
    c = core[0]
    send[HALF] = jnp.zeros_like(send[HALF])
    for j in range(HALF):
        send[j, :PACKED] = packed[j]

    def body(mine):
        for j in range(HALF):
            s = mine * HALF + j
            own, got = offset[s], offset_sib[j, :BS]
            first, second, t1 = (own, got, sib[j, :BS, :BS]) if mine == 0 else (got, own, transfer[s, :BS, :BS])
            send[j, SHIFT : SHIFT + BS] = (mm3(split(t1), split(first)) + second).astype(BF16)

    pl.when(c == 0)(lambda: body(0))
    pl.when(c == 1)(lambda: body(1))


def chain_kernel(recv, prefix, shifts, total, mat, wide):
    wide[...] = jnp.zeros_like(wide)
    product, state = None, None
    for k in range(RUN):
        a = unpack(recv, (k,), mat.at[k])
        b = recv[k, SHIFT : SHIFT + BS].astype(F32)
        if k == 0:
            product, state = a, b
        else:
            product, state = split(mm3(a, product)), mm3(a, split(state)) + b
        if k < RUN - 1:
            prefix[k, 0], prefix[k, 1] = product
            shifts[k] = state
    pack(total, (), product, wide)
    pack_shift(total, (), state)


def state_kernel(place, totals, prefix, shifts, send, state, mat):
    x = place[0]
    first = jnp.full((BS, NRHS), x, jnp.int32) > 0
    state[...] = jnp.where(first, unpack_shift(totals, (0,)), 0.0)
    for g in range(1, GROUPS - 1):

        @pl.when(x > g)
        def _(g=g):
            state[...] = mm3(unpack(totals, (g,), mat), split(state[...])) + unpack_shift(totals, (g,))

    inflow = split(state[...])
    send[0, :BS] = inflow[0]
    for k in range(1, RUN):
        send[k, :BS] = (mm3((prefix[k - 1, 0], prefix[k - 1, 1]), inflow) + shifts[k - 1]).astype(BF16)


def half_kernel(core, transfer, offset, sib, offset_sib, inflow, out, send):
    c = core[0]

    def body(mine):
        for j in range(HALF):
            s = mine * HALF + j
            t, o = split(transfer[s, :BS, :BS]), offset[s]
            v = inflow[j, :BS]
            if mine == 0:
                out[j] = o + (mm(t[0], v) + mm(t[1], v))
                send[j, :BS] = out[j].astype(BF16)
            else:
                first = split(sib[j, :BS, :BS])
                middle = offset_sib[j, :BS] + (mm(first[0], v) + mm(first[1], v))
                out[j] = o + mm3(t, split(middle))
                send[j, :BS] = v

    pl.when(c == 0)(lambda: body(0))
    pl.when(c == 1)(lambda: body(1))


def final_kernel(core, transfer, offset, half, inflow, out):
    c = core[0]

    def body(mine):
        for j in range(HALF):
            s = mine * HALF + j
            out[s * BS : (s + 1) * BS, 0] = half[j]
        for j in range(HALF):
            s = (1 - mine) * HALF + j
            t, v = split(transfer[s, :BS, :BS]), inflow[j, :BS]
            out[s * BS : (s + 1) * BS, 0] = offset[s] + (mm(t[0], v) + mm(t[1], v))

    pl.when(c == 0)(lambda: body(0))
    pl.when(c == 1)(lambda: body(1))


VMEM = pl.BlockSpec(memory_space=pltpu.VMEM)
SMEM = pl.BlockSpec(memory_space=pltpu.SMEM)
PARAMS = pltpu.CompilerParams(vmem_limit_bytes=20 << 20)


def hbm(*dims, dtype=F32):
    return jax.ShapeDtypeStruct(dims, dtype)


def vmem(*dims, dtype=F32):
    return pltpu.VMEM(dims, dtype)


def call(kernel, outs, args, scratch=()):
    scalar = [a.dtype == jnp.int32 for a in args]
    args = [a if one else pltpu.with_memory_space_constraint(a, pltpu.VMEM) for a, one in zip(args, scalar)]
    return pl.pallas_call(
        kernel,
        out_shape=outs,
        in_specs=[SMEM if one else VMEM for one in scalar],
        out_specs=jax.tree.map(lambda _: VMEM, outs, is_leaf=lambda o: not isinstance(o, tuple)),
        scratch_shapes=scratch,
        compiler_params=PARAMS,
    )(*args)


def local(inverses, couplings, rhs, previous, slot_layer):
    inv, rhs, prev = inverses[0, 0], rhs[0, 0], previous[0, 0]
    place = lax.axis_index("sweep")
    core = (place % 2).reshape(1).astype(jnp.int32)
    group = (place // (2 * RUN)).reshape(1).astype(jnp.int32)
    n_sweep, n_span = lax.axis_size("sweep"), lax.axis_size("span")
    swap = [(i, i ^ 1) for i in range(n_sweep)]
    wide = pltpu.VMEM((2, SECOND, 2 * LANE), F32)

    lower = lax.ppermute(prev, "span", [(i, (i + 1) % n_span) for i in range(n_span)])
    upper = lax.ppermute(prev, "span", [((i + 1) % n_span, i) for i in range(n_span)])
    down = lax.ppermute(prev, "sweep", [(i + 1, i) for i in range(n_sweep - 1)])

    anywhere = pl.BlockSpec(memory_space=pl.ANY)
    whole = [pltpu.with_memory_space_constraint(a, pltpu.HBM) for a in (slot_layer, inv, couplings, rhs, prev)]
    inv, c1, transfer, send, partial = pl.pallas_call(
        local_kernel,
        out_shape=(
            vmem(NZ, BS, BS, dtype=BF16),
            vmem(NZ, BS, BS, dtype=BF16),
            vmem(NZ, ROWS, 2 * LANE),
            hbm(HALF, ROWS, 2 * LANE),
            vmem(NZ, BS, NRHS),
        ),
        in_specs=[SMEM] + [anywhere] * 5,
        out_specs=(VMEM,) * 5,
        scratch_shapes=[
            pltpu.SMEM((1, 1, NZ), jnp.int32),
            pltpu.VMEM((NZ, BS, BS), BF16),
            pltpu.VMEM((2, NZ, BS, BS), BF16),
            pltpu.VMEM((NZ, BS, NRHS), BF16),
            pltpu.VMEM((NZ, BS, NRHS), BF16),
            pltpu.SemaphoreType.DMA((8,)),
        ],
        name="local_kernel",
        compiler_params=PARAMS,
    )(core, *whole)
    sib = lax.ppermute(send, "sweep", swap)
    packed = call(product_kernel, vmem(HALF, PACKED, LANE, dtype=BF16), [core, transfer, sib], [wide])
    partial = pl.pallas_call(
        span_kernel,
        out_shape=vmem(NZ, BS, NRHS),
        in_specs=[anywhere] + [VMEM] * 3,
        out_specs=VMEM,
        scratch_shapes=[pltpu.VMEM((2, NZ, BS, BS), BF16), pltpu.SemaphoreType.DMA((2,))],
        name="span_kernel",
        compiler_params=PARAMS,
    )(whole[2], *(pltpu.with_memory_space_constraint(a, pltpu.VMEM) for a in (partial, lower, upper)))
    offset, send = call(
        offset_kernel,
        (vmem(NZ, BS, NRHS), vmem(HALF, ROWS, NRHS)),
        [core, inv, c1, partial, down],
    )
    offset_sib = lax.ppermute(send, "sweep", swap)
    send = call(
        pair_kernel, vmem(RUN, CHIP, LANE, dtype=BF16), [core, packed, transfer, sib, offset, offset_sib]
    )
    maps = lax.all_to_all(send, "sweep", 0, 0, axis_index_groups=RUNS)
    prefix, shifts, total = call(
        chain_kernel,
        (
            vmem(RUN - 1, 2, BS, BS, dtype=BF16),
            vmem(RUN - 1, BS, NRHS),
            vmem(AFFINE, LANE, dtype=BF16),
        ),
        [maps],
        [pltpu.VMEM((RUN, 2, SECOND, 2 * LANE), BF16), wide],
    )
    totals = lax.all_gather(total, "sweep", axis_index_groups=ACROSS)
    back = call(
        state_kernel,
        vmem(RUN, ROWS, NRHS, dtype=BF16),
        [group, totals, prefix, shifts],
        [pltpu.VMEM((BS, NRHS), F32), pltpu.VMEM((2, SECOND, 2 * LANE), BF16)],
    )
    inflow = lax.all_to_all(back, "sweep", 0, 0, axis_index_groups=RUNS)
    half, send = call(
        half_kernel,
        (vmem(HALF, BS, NRHS), vmem(HALF, ROWS, NRHS, dtype=BF16)),
        [core, transfer, offset, sib, offset_sib, inflow],
    )
    inflow = lax.ppermute(send, "sweep", swap)
    out = call(final_kernel, hbm(NZ * BS, 1, NRHS), [core, transfer, offset, half, inflow])
    return out.reshape(1, 1, NZ, BS, NRHS)


def solution(mesh):
    return jax.shard_map(
        local,
        mesh=mesh,
        in_specs=(
            P("sweep", "span", None, None, None),
            P(None, "sweep", "span", None, None, None),
            P("sweep", "span", None, None, None),
            P("sweep", "span", None, None, None),
            P("sweep", "span", None),
        ),
        out_specs=P("sweep", "span", None, None, None),
        check_vma=False,
    )
```

```python
import jax
import jax.numpy as jnp
from jax import lax
from jax.experimental import pallas as pl
from jax.experimental.pallas import tpu as pltpu
from jax.sharding import PartitionSpec as P


BS, NRHS, NZ = 135, 128, 6
LANE = 128
HALF = NZ // 2
RUN = 4
GROUPS = 4
ROWS = 136
SECOND, TAILS, FOLD = 144, 288, 24
PACKED = TAILS + FOLD
F32, BF16 = jnp.float32, jnp.bfloat16

RUNS = [[(g * RUN + m) * 2 + c for m in range(RUN)] for g in range(GROUPS) for c in range(2)]
ACROSS = [[(g * RUN + m) * 2 + c for g in range(GROUPS)] for m in range(RUN) for c in range(2)]
SHIFT = PACKED + 8
LOW = SHIFT + SECOND
CHIP = SHIFT + ROWS
AFFINE = LOW + ROWS


def mm(a, b):
    return jnp.dot(a, b, preferred_element_type=F32)


def split(v):
    hi = v.astype(BF16)
    return hi, (v - hi.astype(F32)).astype(BF16)


def mm3(a, b):
    return mm(a[0], b[0]) + (mm(a[0], b[1]) + mm(a[1], b[0]))


def pack(ref, at, pair, scratch):
    for k in range(2):
        ref[at + (slice(k * SECOND, k * SECOND + BS),)] = pair[k][:, :LANE].astype(BF16)
        scratch[k, :BS, :BS] = pair[k].astype(F32)
    both = scratch[0, :, LANE:] + pltpu.roll(scratch[1, :, LANE:], 8, 1)
    fold = both[:FOLD]
    for g in range(1, SECOND // FOLD):
        fold = fold + pltpu.roll(both[g * FOLD : (g + 1) * FOLD], 16 * g, 1)
    ref[at + (slice(TAILS, PACKED),)] = fold.astype(BF16)


def unpack(ref, at, scratch):
    fold = ref[at + (slice(TAILS, PACKED),)].astype(F32)
    lane = lax.broadcasted_iota(jnp.int32, fold.shape, 1)
    for g in range(SECOND // FOLD):
        rows = slice(g * FOLD, (g + 1) * FOLD)
        for k in range(2):
            shift = (2 * LANE - 16 * g - 8 * k) % LANE
            part = pltpu.roll(fold, shift, 1) if shift else fold
            scratch[k, rows, LANE:] = jnp.where(lane < 8, part, 0.0).astype(BF16)
    for k in range(2):
        scratch[k, :BS, :LANE] = ref[at + (slice(k * SECOND, k * SECOND + BS),)]
    return scratch[0, :BS, :BS], scratch[1, :BS, :BS]


def pack_shift(ref, at, value):
    ref[at + (slice(SHIFT, SHIFT + BS),)], ref[at + (slice(LOW, LOW + BS),)] = split(value)


def unpack_shift(ref, at):
    return ref[at + (slice(SHIFT, SHIFT + BS),)].astype(F32) + ref[at + (slice(LOW, LOW + BS),)].astype(F32)


def local_kernel(place, layers_in, inv_in, c_in, rhs_in, prev_in, inv, c1, transfer, send, partial, layers, c0, walls, rhs, prev, sems):
    moves = (
        (inv_in, inv),
        (c_in.at[0, 0, 0], c0),
        (prev_in, prev),
        (rhs_in, rhs),
        (layers_in, layers),
        (c_in.at[4, 0, 0], walls.at[0]),
        (c_in.at[5, 0, 0], walls.at[1]),
        (c_in.at[1, 0, 0], c1),
    )
    copies = [pltpu.make_async_copy(source, target, sems.at[i]) for i, (source, target) in enumerate(moves)]
    for copy in copies:
        copy.start()
    for copy in copies[:2]:
        copy.wait()
    for s in range(NZ):
        transfer[s, :BS, :BS] = -mm(inv[s], c0[s])
    other = HALF * (1 - place[0] % 2)
    for j in range(HALF):
        send[j] = transfer[other + j]
    for copy in copies[2:7]:
        copy.wait()
    for s in range(NZ):
        layer = layers[0, 0, s]
        total = rhs[s].astype(F32)
        for step, index in ((-1, 0), (1, 1)):
            found, exists = 0, 0
            for t in range(NZ):
                match = layers[0, 0, t] == layer + step
                found = jnp.where(match, t, found)
                exists = jnp.where(match, 1, exists)
            keep = jnp.full((BS, NRHS), exists, jnp.int32) > 0
            vectors = jnp.where(keep, prev[found].astype(F32), 0.0).astype(BF16)
            total = total - mm(walls[index, s], vectors)
        partial[s] = total
    for copy in copies[7:]:
        copy.wait()


def product_kernel(place, transfer, sib, packed, wide):
    c = place[0] % 2
    wide[...] = jnp.zeros_like(wide)

    def body(mine):
        for j in range(HALF):
            own, got = split(transfer[mine * HALF + j, :BS, :BS]), split(sib[j, :BS, :BS])
            pack(packed, (j,), split(mm3(got, own) if mine == 0 else mm3(own, got)), wide)

    pl.when(c == 0)(lambda: body(0))
    pl.when(c == 1)(lambda: body(1))


def span_kernel(c_in, partial, lower, upper, out, c, sems):
    copies = [pltpu.make_async_copy(c_in.at[2 + i, 0, 0], c.at[i], sems.at[i]) for i in range(2)]
    for copy in copies:
        copy.start()
    copies[0].wait()
    for s in range(NZ):
        out[s] = partial[s] - mm(c[0, s], lower[s])
    copies[1].wait()
    for s in range(NZ):
        out[s] = out[s] - mm(c[1, s], upper[s])


def offset_kernel(place, inv, c1, partial, down, out, send):
    for s in range(NZ):
        forcing = (partial[s] - mm(c1[s], down[s])).astype(BF16)
        out[s] = mm(inv[s], forcing)
    other = HALF * (1 - place[0] % 2)
    for j in range(HALF):
        send[j, :BS] = out[other + j]


def pair_kernel(place, packed, transfer, sib, offset, offset_sib, send):
    c = place[0] % 2
    send[HALF] = jnp.zeros_like(send[HALF])
    for j in range(HALF):
        send[j, :PACKED] = packed[j]

    def body(mine):
        for j in range(HALF):
            s = mine * HALF + j
            own, got = offset[s], offset_sib[j, :BS]
            first, second, t1 = (own, got, sib[j, :BS, :BS]) if mine == 0 else (got, own, transfer[s, :BS, :BS])
            send[j, SHIFT : SHIFT + BS] = (mm3(split(t1), split(first)) + second).astype(BF16)

    pl.when(c == 0)(lambda: body(0))
    pl.when(c == 1)(lambda: body(1))


def chain_kernel(recv, prefix, shifts, total, mat, wide):
    wide[...] = jnp.zeros_like(wide)
    product, state = None, None
    for k in range(RUN):
        a = unpack(recv, (k,), mat.at[k])
        b = recv[k, SHIFT : SHIFT + BS].astype(F32)
        if k == 0:
            product, state = a, b
        else:
            product, state = split(mm3(a, product)), mm3(a, split(state)) + b
        if k < RUN - 1:
            prefix[k, 0], prefix[k, 1] = product
            shifts[k] = state
    pack(total, (), product, wide)
    pack_shift(total, (), state)


def state_kernel(place, totals, prefix, shifts, send, state, mat):
    x = place[0] // (2 * RUN)
    first = jnp.full((BS, NRHS), x, jnp.int32) > 0
    state[...] = jnp.where(first, unpack_shift(totals, (0,)), 0.0)
    for g in range(1, GROUPS - 1):

        @pl.when(x > g)
        def _(g=g):
            state[...] = mm3(unpack(totals, (g,), mat), split(state[...])) + unpack_shift(totals, (g,))

    inflow = split(state[...])
    send[0, :BS] = inflow[0]
    for k in range(1, RUN):
        send[k, :BS] = (mm3((prefix[k - 1, 0], prefix[k - 1, 1]), inflow) + shifts[k - 1]).astype(BF16)


def relay_kernel(place, transfer, offset, inflow, send):
    c = place[0] % 2

    @pl.when(c == 0)
    def _():
        for j in range(HALF):
            t, v = split(transfer[j, :BS, :BS]), inflow[j, :BS]
            send[j, :BS] = (offset[j] + (mm(t[0], v) + mm(t[1], v))).astype(BF16)

    @pl.when(c == 1)
    def _():
        for j in range(HALF):
            send[j, :BS] = inflow[j, :BS]


def half_kernel(place, transfer, offset, sib, offset_sib, inflow, out):
    c = place[0] % 2

    def body(mine):
        for j in range(HALF):
            s = mine * HALF + j
            t, v = split(transfer[s, :BS, :BS]), inflow[j, :BS]
            if mine == 0:
                out[j] = offset[s] + (mm(t[0], v) + mm(t[1], v))
            else:
                first = split(sib[j, :BS, :BS])
                middle = offset_sib[j, :BS] + (mm(first[0], v) + mm(first[1], v))
                out[j] = offset[s] + mm3(t, split(middle))

    pl.when(c == 0)(lambda: body(0))
    pl.when(c == 1)(lambda: body(1))


def final_kernel(place, transfer, offset, half, inflow, out):
    c = place[0] % 2

    def body(mine):
        for j in range(HALF):
            s = mine * HALF + j
            out[s * BS : (s + 1) * BS, 0] = half[j]
        for j in range(HALF):
            s = (1 - mine) * HALF + j
            t, v = split(transfer[s, :BS, :BS]), inflow[j, :BS]
            out[s * BS : (s + 1) * BS, 0] = offset[s] + (mm(t[0], v) + mm(t[1], v))

    pl.when(c == 0)(lambda: body(0))
    pl.when(c == 1)(lambda: body(1))


VMEM = pl.BlockSpec(memory_space=pltpu.VMEM)
SMEM = pl.BlockSpec(memory_space=pltpu.SMEM)
PARAMS = pltpu.CompilerParams(vmem_limit_bytes=20 << 20)


def hbm(*dims, dtype=F32):
    return jax.ShapeDtypeStruct(dims, dtype)


def vmem(*dims, dtype=F32):
    return pltpu.VMEM(dims, dtype)


def call(kernel, outs, args, scratch=()):
    scalar = [a.dtype == jnp.int32 for a in args]
    args = [a if one else pltpu.with_memory_space_constraint(a, pltpu.VMEM) for a, one in zip(args, scalar)]
    return pl.pallas_call(
        kernel,
        out_shape=outs,
        in_specs=[SMEM if one else VMEM for one in scalar],
        out_specs=jax.tree.map(lambda _: VMEM, outs, is_leaf=lambda o: not isinstance(o, tuple)),
        scratch_shapes=scratch,
        compiler_params=PARAMS,
    )(*args)


def local(inverses, couplings, rhs, previous, slot_layer):
    inv, rhs, prev = inverses[0, 0], rhs[0, 0], previous[0, 0]
    place = lax.axis_index("sweep").reshape(1).astype(jnp.int32)
    n_sweep, n_span = lax.axis_size("sweep"), lax.axis_size("span")
    swap = [(i, i ^ 1) for i in range(n_sweep)]
    wide = pltpu.VMEM((2, SECOND, 2 * LANE), F32)

    lower = lax.ppermute(prev, "span", [(i, (i + 1) % n_span) for i in range(n_span)])
    upper = lax.ppermute(prev, "span", [((i + 1) % n_span, i) for i in range(n_span)])
    down = lax.ppermute(prev, "sweep", [(i + 1, i) for i in range(n_sweep - 1)])

    anywhere = pl.BlockSpec(memory_space=pl.ANY)
    whole = [pltpu.with_memory_space_constraint(a, pltpu.HBM) for a in (slot_layer, inv, couplings, rhs, prev)]
    inv, c1, transfer, send, partial = pl.pallas_call(
        local_kernel,
        out_shape=(
            vmem(NZ, BS, BS, dtype=BF16),
            vmem(NZ, BS, BS, dtype=BF16),
            vmem(NZ, ROWS, 2 * LANE),
            hbm(HALF, ROWS, 2 * LANE),
            vmem(NZ, BS, NRHS),
        ),
        in_specs=[SMEM] + [anywhere] * 5,
        out_specs=(VMEM,) * 5,
        scratch_shapes=[
            pltpu.SMEM((1, 1, NZ), jnp.int32),
            pltpu.VMEM((NZ, BS, BS), BF16),
            pltpu.VMEM((2, NZ, BS, BS), BF16),
            pltpu.VMEM((NZ, BS, NRHS), BF16),
            pltpu.VMEM((NZ, BS, NRHS), BF16),
            pltpu.SemaphoreType.DMA((8,)),
        ],
        name="local_kernel",
        compiler_params=PARAMS,
    )(place, *whole)
    sib = lax.ppermute(send, "sweep", swap)
    packed = call(product_kernel, vmem(HALF, PACKED, LANE, dtype=BF16), [place, transfer, sib], [wide])
    partial = pl.pallas_call(
        span_kernel,
        out_shape=vmem(NZ, BS, NRHS),
        in_specs=[anywhere] + [VMEM] * 3,
        out_specs=VMEM,
        scratch_shapes=[pltpu.VMEM((2, NZ, BS, BS), BF16), pltpu.SemaphoreType.DMA((2,))],
        name="span_kernel",
        compiler_params=PARAMS,
    )(whole[2], *(pltpu.with_memory_space_constraint(a, pltpu.VMEM) for a in (partial, lower, upper)))
    offset, send = call(
        offset_kernel,
        (vmem(NZ, BS, NRHS), vmem(HALF, ROWS, NRHS)),
        [place, inv, c1, partial, down],
    )
    offset_sib = lax.ppermute(send, "sweep", swap)
    send = call(
        pair_kernel, vmem(RUN, CHIP, LANE, dtype=BF16), [place, packed, transfer, sib, offset, offset_sib]
    )
    maps = lax.all_to_all(send, "sweep", 0, 0, axis_index_groups=RUNS)
    prefix, shifts, total = call(
        chain_kernel,
        (
            vmem(RUN - 1, 2, BS, BS, dtype=BF16),
            vmem(RUN - 1, BS, NRHS),
            vmem(AFFINE, LANE, dtype=BF16),
        ),
        [maps],
        [pltpu.VMEM((RUN, 2, SECOND, 2 * LANE), BF16), wide],
    )
    totals = lax.all_gather(total, "sweep", axis_index_groups=ACROSS)
    back = call(
        state_kernel,
        vmem(RUN, ROWS, NRHS, dtype=BF16),
        [place, totals, prefix, shifts],
        [pltpu.VMEM((BS, NRHS), F32), pltpu.VMEM((2, SECOND, 2 * LANE), BF16)],
    )
    inflow = lax.all_to_all(back, "sweep", 0, 0, axis_index_groups=RUNS)
    send = call(relay_kernel, vmem(HALF, ROWS, NRHS, dtype=BF16), [place, transfer, offset, inflow])
    half = call(half_kernel, vmem(HALF, BS, NRHS), [place, transfer, offset, sib, offset_sib, inflow])
    inflow = lax.ppermute(send, "sweep", swap)
    out = call(final_kernel, hbm(NZ * BS, 1, NRHS), [place, transfer, offset, half, inflow])
    return out.reshape(1, 1, NZ, BS, NRHS)


def solution(mesh):
    return jax.shard_map(
        local,
        mesh=mesh,
        in_specs=(
            P("sweep", "span", None, None, None),
            P(None, "sweep", "span", None, None, None),
            P("sweep", "span", None, None, None),
            P("sweep", "span", None, None, None),
            P("sweep", "span", None),
        ),
        out_specs=P("sweep", "span", None, None, None),
        check_vma=False,
    )
```

```python
import jax
import jax.numpy as jnp
from jax import lax
from jax.experimental import pallas as pl
from jax.experimental.pallas import tpu as pltpu
from jax.sharding import PartitionSpec as P


BS, NRHS, NZ = 135, 128, 6
LANE = 128
HALF = NZ // 2
RUN = 4
GROUPS = 4
ROWS = 136
SECOND, TAILS, FOLD = 144, 288, 24
PACKED = TAILS + FOLD
F32, BF16 = jnp.float32, jnp.bfloat16

RUNS = [[(g * RUN + m) * 2 + c for m in range(RUN)] for g in range(GROUPS) for c in range(2)]
ACROSS = [[(g * RUN + m) * 2 + c for g in range(GROUPS)] for m in range(RUN) for c in range(2)]
SHIFT = PACKED + 8
LOW = SHIFT + SECOND
CHIP = SHIFT + ROWS
AFFINE = LOW + ROWS


def mm(a, b):
    return jnp.dot(a, b, preferred_element_type=F32)


def split(v):
    hi = v.astype(BF16)
    return hi, (v - hi.astype(F32)).astype(BF16)


def mm3(a, b):
    return mm(a[0], b[0]) + (mm(a[0], b[1]) + mm(a[1], b[0]))


def pack(ref, at, pair, scratch):
    for k in range(2):
        ref[at + (slice(k * SECOND, k * SECOND + BS),)] = pair[k][:, :LANE].astype(BF16)
        scratch[k, :BS, :BS] = pair[k].astype(F32)
    both = scratch[0, :, LANE:] + pltpu.roll(scratch[1, :, LANE:], 8, 1)
    fold = both[:FOLD]
    for g in range(1, SECOND // FOLD):
        fold = fold + pltpu.roll(both[g * FOLD : (g + 1) * FOLD], 16 * g, 1)
    ref[at + (slice(TAILS, PACKED),)] = fold.astype(BF16)


def unpack(ref, at, scratch):
    fold = ref[at + (slice(TAILS, PACKED),)].astype(F32)
    lane = lax.broadcasted_iota(jnp.int32, fold.shape, 1)
    for g in range(SECOND // FOLD):
        rows = slice(g * FOLD, (g + 1) * FOLD)
        for k in range(2):
            shift = (2 * LANE - 16 * g - 8 * k) % LANE
            part = pltpu.roll(fold, shift, 1) if shift else fold
            scratch[k, rows, LANE:] = jnp.where(lane < 8, part, 0.0).astype(BF16)
    for k in range(2):
        scratch[k, :BS, :LANE] = ref[at + (slice(k * SECOND, k * SECOND + BS),)]
    return scratch[0, :BS, :BS], scratch[1, :BS, :BS]


def pack_shift(ref, at, value):
    ref[at + (slice(SHIFT, SHIFT + BS),)], ref[at + (slice(LOW, LOW + BS),)] = split(value)


def unpack_shift(ref, at):
    return ref[at + (slice(SHIFT, SHIFT + BS),)].astype(F32) + ref[at + (slice(LOW, LOW + BS),)].astype(F32)


def local_kernel(place, layers_in, inv_in, c_in, rhs_in, prev_in, inv, last, transfer, send, partial, layers, c0, walls, rhs, prev, sems):
    moves = (
        (inv_in, inv),
        (c_in.at[0, 0, 0], c0),
        (prev_in, prev),
        (rhs_in, rhs),
        (layers_in, layers),
        (c_in.at[4, 0, 0], walls.at[0]),
        (c_in.at[5, 0, 0], walls.at[1]),
        (c_in.at[3, 0, 0], last),
    )
    copies = [pltpu.make_async_copy(source, target, sems.at[i]) for i, (source, target) in enumerate(moves)]
    for copy in copies:
        copy.start()
    for copy in copies[:2]:
        copy.wait()
    for s in range(NZ):
        transfer[s, :BS, :BS] = -mm(inv[s], c0[s])
    other = HALF * (1 - place[0] % 2)
    for j in range(HALF):
        send[j] = transfer[other + j]
    for copy in copies[2:7]:
        copy.wait()
    for s in range(NZ):
        layer = layers[0, 0, s]
        total = rhs[s].astype(F32)
        for step, index in ((-1, 0), (1, 1)):
            found, exists = 0, 0
            for t in range(NZ):
                match = layers[0, 0, t] == layer + step
                found = jnp.where(match, t, found)
                exists = jnp.where(match, 1, exists)
            keep = jnp.full((BS, NRHS), exists, jnp.int32) > 0
            vectors = jnp.where(keep, prev[found].astype(F32), 0.0).astype(BF16)
            total = total - mm(walls[index, s], vectors)
        partial[s] = total
    for copy in copies[7:]:
        copy.wait()


def product_kernel(place, transfer, sib, packed, wide):
    c = place[0] % 2
    wide[...] = jnp.zeros_like(wide)

    def body(mine):
        for j in range(HALF):
            own, got = split(transfer[mine * HALF + j, :BS, :BS]), split(sib[j, :BS, :BS])
            pack(packed, (j,), split(mm3(got, own) if mine == 0 else mm3(own, got)), wide)

    pl.when(c == 0)(lambda: body(0))
    pl.when(c == 1)(lambda: body(1))


def early_kernel(c_in, partial, down, lower, out, c, sems):
    copies = [pltpu.make_async_copy(c_in.at[1 + i, 0, 0], c.at[i], sems.at[i]) for i in range(2)]
    for copy in copies:
        copy.start()
    copies[0].wait()
    for s in range(NZ):
        out[s] = partial[s] - mm(c[0, s], down[s])
    copies[1].wait()
    for s in range(NZ):
        out[s] = out[s] - mm(c[1, s], lower[s])


def offset_kernel(place, inv, c, partial, upper, out, send):
    for s in range(NZ):
        forcing = (partial[s] - mm(c[s], upper[s])).astype(BF16)
        out[s] = mm(inv[s], forcing)
    other = HALF * (1 - place[0] % 2)
    for j in range(HALF):
        send[j, :BS] = out[other + j]


def pair_kernel(place, packed, transfer, sib, offset, offset_sib, send):
    c = place[0] % 2
    send[HALF] = jnp.zeros_like(send[HALF])
    for j in range(HALF):
        send[j, :PACKED] = packed[j]

    def body(mine):
        for j in range(HALF):
            s = mine * HALF + j
            own, got = offset[s], offset_sib[j, :BS]
            first, second, t1 = (own, got, sib[j, :BS, :BS]) if mine == 0 else (got, own, transfer[s, :BS, :BS])
            send[j, SHIFT : SHIFT + BS] = (mm3(split(t1), split(first)) + second).astype(BF16)

    pl.when(c == 0)(lambda: body(0))
    pl.when(c == 1)(lambda: body(1))


def chain_kernel(recv, prefix, shifts, total, mat, wide):
    wide[...] = jnp.zeros_like(wide)
    product, state = None, None
    for k in range(RUN):
        a = unpack(recv, (k,), mat.at[k])
        b = recv[k, SHIFT : SHIFT + BS].astype(F32)
        if k == 0:
            product, state = a, b
        else:
            product, state = split(mm3(a, product)), mm3(a, split(state)) + b
        if k < RUN - 1:
            prefix[k, 0], prefix[k, 1] = product
            shifts[k] = state
    pack(total, (), product, wide)
    pack_shift(total, (), state)


def state_kernel(place, totals, prefix, shifts, send, state, mat):
    x = place[0] // (2 * RUN)
    first = jnp.full((BS, NRHS), x, jnp.int32) > 0
    state[...] = jnp.where(first, unpack_shift(totals, (0,)), 0.0)
    for g in range(1, GROUPS - 1):

        @pl.when(x > g)
        def _(g=g):
            state[...] = mm3(unpack(totals, (g,), mat), split(state[...])) + unpack_shift(totals, (g,))

    inflow = split(state[...])
    send[0, :BS] = inflow[0]
    for k in range(1, RUN):
        send[k, :BS] = (mm3((prefix[k - 1, 0], prefix[k - 1, 1]), inflow) + shifts[k - 1]).astype(BF16)


def relay_kernel(place, transfer, offset, inflow, send):
    c = place[0] % 2

    @pl.when(c == 0)
    def _():
        for j in range(HALF):
            t, v = split(transfer[j, :BS, :BS]), inflow[j, :BS]
            send[j, :BS] = (offset[j] + (mm(t[0], v) + mm(t[1], v))).astype(BF16)

    @pl.when(c == 1)
    def _():
        for j in range(HALF):
            send[j, :BS] = inflow[j, :BS]


def half_kernel(place, transfer, offset, sib, offset_sib, inflow, out):
    c = place[0] % 2

    def body(mine):
        for j in range(HALF):
            s = mine * HALF + j
            t, v = split(transfer[s, :BS, :BS]), inflow[j, :BS]
            if mine == 0:
                out[j] = offset[s] + (mm(t[0], v) + mm(t[1], v))
            else:
                first = split(sib[j, :BS, :BS])
                middle = offset_sib[j, :BS] + (mm(first[0], v) + mm(first[1], v))
                out[j] = offset[s] + mm3(t, split(middle))

    pl.when(c == 0)(lambda: body(0))
    pl.when(c == 1)(lambda: body(1))


def final_kernel(place, transfer, offset, half, inflow, out):
    c = place[0] % 2

    def body(mine):
        for j in range(HALF):
            s = mine * HALF + j
            out[s * BS : (s + 1) * BS, 0] = half[j]
        for j in range(HALF):
            s = (1 - mine) * HALF + j
            t, v = split(transfer[s, :BS, :BS]), inflow[j, :BS]
            out[s * BS : (s + 1) * BS, 0] = offset[s] + (mm(t[0], v) + mm(t[1], v))

    pl.when(c == 0)(lambda: body(0))
    pl.when(c == 1)(lambda: body(1))


VMEM = pl.BlockSpec(memory_space=pltpu.VMEM)
SMEM = pl.BlockSpec(memory_space=pltpu.SMEM)
PARAMS = pltpu.CompilerParams(vmem_limit_bytes=20 << 20)


def hbm(*dims, dtype=F32):
    return jax.ShapeDtypeStruct(dims, dtype)


def vmem(*dims, dtype=F32):
    return pltpu.VMEM(dims, dtype)


def call(kernel, outs, args, scratch=()):
    scalar = [a.dtype == jnp.int32 for a in args]
    args = [a if one else pltpu.with_memory_space_constraint(a, pltpu.VMEM) for a, one in zip(args, scalar)]
    return pl.pallas_call(
        kernel,
        out_shape=outs,
        in_specs=[SMEM if one else VMEM for one in scalar],
        out_specs=jax.tree.map(lambda _: VMEM, outs, is_leaf=lambda o: not isinstance(o, tuple)),
        scratch_shapes=scratch,
        compiler_params=PARAMS,
    )(*args)


def local(inverses, couplings, rhs, previous, slot_layer):
    inv, rhs, prev = inverses[0, 0], rhs[0, 0], previous[0, 0]
    place = lax.axis_index("sweep").reshape(1).astype(jnp.int32)
    n_sweep, n_span = lax.axis_size("sweep"), lax.axis_size("span")
    swap = [(i, i ^ 1) for i in range(n_sweep)]
    wide = pltpu.VMEM((2, SECOND, 2 * LANE), F32)

    lower = lax.ppermute(prev, "span", [(i, (i + 1) % n_span) for i in range(n_span)])
    upper = lax.ppermute(prev, "span", [((i + 1) % n_span, i) for i in range(n_span)])
    down = lax.ppermute(prev, "sweep", [(i + 1, i) for i in range(n_sweep - 1)])

    anywhere = pl.BlockSpec(memory_space=pl.ANY)
    whole = [pltpu.with_memory_space_constraint(a, pltpu.HBM) for a in (slot_layer, inv, couplings, rhs, prev)]
    inv, last, transfer, send, partial = pl.pallas_call(
        local_kernel,
        out_shape=(
            vmem(NZ, BS, BS, dtype=BF16),
            vmem(NZ, BS, BS, dtype=BF16),
            vmem(NZ, ROWS, 2 * LANE),
            hbm(HALF, ROWS, 2 * LANE),
            vmem(NZ, BS, NRHS),
        ),
        in_specs=[SMEM] + [anywhere] * 5,
        out_specs=(VMEM,) * 5,
        scratch_shapes=[
            pltpu.SMEM((1, 1, NZ), jnp.int32),
            pltpu.VMEM((NZ, BS, BS), BF16),
            pltpu.VMEM((2, NZ, BS, BS), BF16),
            pltpu.VMEM((NZ, BS, NRHS), BF16),
            pltpu.VMEM((NZ, BS, NRHS), BF16),
            pltpu.SemaphoreType.DMA((8,)),
        ],
        name="local_kernel",
        compiler_params=PARAMS,
    )(place, *whole)
    sib = lax.ppermute(send, "sweep", swap)
    packed = call(product_kernel, vmem(HALF, PACKED, LANE, dtype=BF16), [place, transfer, sib], [wide])
    partial = pl.pallas_call(
        early_kernel,
        out_shape=vmem(NZ, BS, NRHS),
        in_specs=[anywhere] + [VMEM] * 3,
        out_specs=VMEM,
        scratch_shapes=[pltpu.VMEM((2, NZ, BS, BS), BF16), pltpu.SemaphoreType.DMA((2,))],
        name="early_kernel",
        compiler_params=PARAMS,
    )(whole[2], *(pltpu.with_memory_space_constraint(a, pltpu.VMEM) for a in (partial, down, lower)))
    offset, send = call(
        offset_kernel,
        (vmem(NZ, BS, NRHS), vmem(HALF, ROWS, NRHS)),
        [place, inv, last, partial, upper],
    )
    offset_sib = lax.ppermute(send, "sweep", swap)
    send = call(
        pair_kernel, vmem(RUN, CHIP, LANE, dtype=BF16), [place, packed, transfer, sib, offset, offset_sib]
    )
    maps = lax.all_to_all(send, "sweep", 0, 0, axis_index_groups=RUNS)
    prefix, shifts, total = call(
        chain_kernel,
        (
            vmem(RUN - 1, 2, BS, BS, dtype=BF16),
            vmem(RUN - 1, BS, NRHS),
            vmem(AFFINE, LANE, dtype=BF16),
        ),
        [maps],
        [pltpu.VMEM((RUN, 2, SECOND, 2 * LANE), BF16), wide],
    )
    totals = lax.all_gather(total, "sweep", axis_index_groups=ACROSS)
    back = call(
        state_kernel,
        vmem(RUN, ROWS, NRHS, dtype=BF16),
        [place, totals, prefix, shifts],
        [pltpu.VMEM((BS, NRHS), F32), pltpu.VMEM((2, SECOND, 2 * LANE), BF16)],
    )
    inflow = lax.all_to_all(back, "sweep", 0, 0, axis_index_groups=RUNS)
    send = call(relay_kernel, vmem(HALF, ROWS, NRHS, dtype=BF16), [place, transfer, offset, inflow])
    half = call(half_kernel, vmem(HALF, BS, NRHS), [place, transfer, offset, sib, offset_sib, inflow])
    inflow = lax.ppermute(send, "sweep", swap)
    out = call(final_kernel, hbm(NZ * BS, 1, NRHS), [place, transfer, offset, half, inflow])
    return out.reshape(1, 1, NZ, BS, NRHS)


def solution(mesh):
    return jax.shard_map(
        local,
        mesh=mesh,
        in_specs=(
            P("sweep", "span", None, None, None),
            P(None, "sweep", "span", None, None, None),
            P("sweep", "span", None, None, None),
            P("sweep", "span", None, None, None),
            P("sweep", "span", None),
        ),
        out_specs=P("sweep", "span", None, None, None),
        check_vma=False,
    )
```

```python
import jax
import jax.numpy as jnp
from jax import lax
from jax.experimental import pallas as pl
from jax.experimental.pallas import tpu as pltpu
from jax.sharding import PartitionSpec as P


BS, NRHS, NZ = 135, 128, 6
LANE = 128
HALF = NZ // 2
RUN = 4
GROUPS = 4
ROWS = 136
SECOND, TAILS, FOLD = 144, 288, 24
PACKED = TAILS + FOLD
F32, BF16 = jnp.float32, jnp.bfloat16

RUNS = [[(g * RUN + m) * 2 + c for m in range(RUN)] for g in range(GROUPS) for c in range(2)]
ACROSS = [[(g * RUN + m) * 2 + c for g in range(GROUPS)] for m in range(RUN) for c in range(2)]
SHIFT = PACKED + 8
LOW = SHIFT + SECOND
CHIP = SHIFT + ROWS
AFFINE = LOW + ROWS


def mm(a, b):
    return jnp.dot(a, b, preferred_element_type=F32)


def split(v):
    hi = v.astype(BF16)
    return hi, (v - hi.astype(F32)).astype(BF16)


def mm3(a, b):
    return mm(a[0], b[0]) + (mm(a[0], b[1]) + mm(a[1], b[0]))


def pack(ref, at, pair, scratch):
    for k in range(2):
        ref[at + (slice(k * SECOND, k * SECOND + BS),)] = pair[k][:, :LANE].astype(BF16)
        scratch[k, :BS, :BS] = pair[k].astype(F32)
    both = scratch[0, :, LANE:] + pltpu.roll(scratch[1, :, LANE:], 8, 1)
    fold = both[:FOLD]
    for g in range(1, SECOND // FOLD):
        fold = fold + pltpu.roll(both[g * FOLD : (g + 1) * FOLD], 16 * g, 1)
    ref[at + (slice(TAILS, PACKED),)] = fold.astype(BF16)


def unpack(ref, at, scratch):
    fold = ref[at + (slice(TAILS, PACKED),)].astype(F32)
    lane = lax.broadcasted_iota(jnp.int32, fold.shape, 1)
    for g in range(SECOND // FOLD):
        rows = slice(g * FOLD, (g + 1) * FOLD)
        for k in range(2):
            shift = (2 * LANE - 16 * g - 8 * k) % LANE
            part = pltpu.roll(fold, shift, 1) if shift else fold
            scratch[k, rows, LANE:] = jnp.where(lane < 8, part, 0.0).astype(BF16)
    for k in range(2):
        scratch[k, :BS, :LANE] = ref[at + (slice(k * SECOND, k * SECOND + BS),)]
    return scratch[0, :BS, :BS], scratch[1, :BS, :BS]


def pack_shift(ref, at, value):
    ref[at + (slice(SHIFT, SHIFT + BS),)], ref[at + (slice(LOW, LOW + BS),)] = split(value)


def unpack_shift(ref, at):
    return ref[at + (slice(SHIFT, SHIFT + BS),)].astype(F32) + ref[at + (slice(LOW, LOW + BS),)].astype(F32)


def local_kernel(place, layers_in, inv_in, c_in, rhs_in, prev_in, inv, last, near, transfer, send, partial, layers, c0, walls, rhs, prev, sems):
    moves = (
        (inv_in, inv),
        (c_in.at[0, 0, 0], c0),
        (prev_in, prev),
        (rhs_in, rhs),
        (layers_in, layers),
        (c_in.at[4, 0, 0], walls.at[0]),
        (c_in.at[5, 0, 0], walls.at[1]),
        (c_in.at[1, 0, 0], near),
        (c_in.at[3, 0, 0], last),
    )
    copies = [pltpu.make_async_copy(source, target, sems.at[i]) for i, (source, target) in enumerate(moves)]
    for copy in copies:
        copy.start()
    for copy in copies[:2]:
        copy.wait()
    for s in range(NZ):
        transfer[s, :BS, :BS] = -mm(inv[s], c0[s])
    other = HALF * (1 - place[0] % 2)
    for j in range(HALF):
        send[j] = transfer[other + j]
    for copy in copies[2:7]:
        copy.wait()
    for s in range(NZ):
        layer = layers[0, 0, s]
        total = rhs[s].astype(F32)
        for step, index in ((-1, 0), (1, 1)):
            found, exists = 0, 0
            for t in range(NZ):
                match = layers[0, 0, t] == layer + step
                found = jnp.where(match, t, found)
                exists = jnp.where(match, 1, exists)
            keep = jnp.full((BS, NRHS), exists, jnp.int32) > 0
            vectors = jnp.where(keep, prev[found].astype(F32), 0.0).astype(BF16)
            total = total - mm(walls[index, s], vectors)
        partial[s] = total
    for copy in copies[7:]:
        copy.wait()


def product_kernel(place, transfer, sib, packed, wide):
    c = place[0] % 2
    wide[...] = jnp.zeros_like(wide)

    def body(mine):
        for j in range(HALF):
            own, got = split(transfer[mine * HALF + j, :BS, :BS]), split(sib[j, :BS, :BS])
            pack(packed, (j,), split(mm3(got, own) if mine == 0 else mm3(own, got)), wide)

    pl.when(c == 0)(lambda: body(0))
    pl.when(c == 1)(lambda: body(1))


def early_kernel(c_in, near, partial, down, lower, out, c, sem):
    copy = pltpu.make_async_copy(c_in.at[2, 0, 0], c, sem)
    copy.start()
    for s in range(NZ):
        out[s] = partial[s] - mm(near[s], down[s])
    copy.wait()
    for s in range(NZ):
        out[s] = out[s] - mm(c[s], lower[s])


def offset_kernel(place, inv, c, partial, upper, out, send):
    for s in range(NZ):
        forcing = (partial[s] - mm(c[s], upper[s])).astype(BF16)
        out[s] = mm(inv[s], forcing)
    other = HALF * (1 - place[0] % 2)
    for j in range(HALF):
        send[j, :BS] = out[other + j]


def pair_kernel(place, packed, transfer, sib, offset, offset_sib, send):
    c = place[0] % 2
    send[HALF] = jnp.zeros_like(send[HALF])
    for j in range(HALF):
        send[j, :PACKED] = packed[j]

    def body(mine):
        for j in range(HALF):
            s = mine * HALF + j
            own, got = offset[s], offset_sib[j, :BS]
            first, second, t1 = (own, got, sib[j, :BS, :BS]) if mine == 0 else (got, own, transfer[s, :BS, :BS])
            send[j, SHIFT : SHIFT + BS] = (mm3(split(t1), split(first)) + second).astype(BF16)

    pl.when(c == 0)(lambda: body(0))
    pl.when(c == 1)(lambda: body(1))


def chain_kernel(recv, prefix, shifts, total, mat, wide):
    wide[...] = jnp.zeros_like(wide)
    product, state = None, None
    for k in range(RUN):
        a = unpack(recv, (k,), mat.at[k])
        b = recv[k, SHIFT : SHIFT + BS].astype(F32)
        if k == 0:
            product, state = a, b
        else:
            product, state = split(mm3(a, product)), mm3(a, split(state)) + b
        if k < RUN - 1:
            prefix[k, 0], prefix[k, 1] = product
            shifts[k] = state
    pack(total, (), product, wide)
    pack_shift(total, (), state)


def state_kernel(place, totals, prefix, shifts, send, state, mat):
    x = place[0] // (2 * RUN)
    first = jnp.full((BS, NRHS), x, jnp.int32) > 0
    state[...] = jnp.where(first, unpack_shift(totals, (0,)), 0.0)
    for g in range(1, GROUPS - 1):

        @pl.when(x > g)
        def _(g=g):
            state[...] = mm3(unpack(totals, (g,), mat), split(state[...])) + unpack_shift(totals, (g,))

    inflow = split(state[...])
    send[0, :BS] = inflow[0]
    for k in range(1, RUN):
        send[k, :BS] = (mm3((prefix[k - 1, 0], prefix[k - 1, 1]), inflow) + shifts[k - 1]).astype(BF16)


def relay_kernel(place, transfer, offset, inflow, send):
    c = place[0] % 2

    @pl.when(c == 0)
    def _():
        for j in range(HALF):
            t, v = split(transfer[j, :BS, :BS]), inflow[j, :BS]
            send[j, :BS] = (offset[j] + (mm(t[0], v) + mm(t[1], v))).astype(BF16)

    @pl.when(c == 1)
    def _():
        for j in range(HALF):
            send[j, :BS] = inflow[j, :BS]


def half_kernel(place, transfer, offset, sib, offset_sib, inflow, out):
    c = place[0] % 2

    def body(mine):
        for j in range(HALF):
            s = mine * HALF + j
            t, v = split(transfer[s, :BS, :BS]), inflow[j, :BS]
            if mine == 0:
                out[j] = offset[s] + (mm(t[0], v) + mm(t[1], v))
            else:
                first = split(sib[j, :BS, :BS])
                middle = offset_sib[j, :BS] + (mm(first[0], v) + mm(first[1], v))
                out[j] = offset[s] + mm3(t, split(middle))

    pl.when(c == 0)(lambda: body(0))
    pl.when(c == 1)(lambda: body(1))


def final_kernel(place, transfer, offset, half, inflow, out):
    c = place[0] % 2

    def body(mine):
        for j in range(HALF):
            s = mine * HALF + j
            out[s * BS : (s + 1) * BS, 0] = half[j]
        for j in range(HALF):
            s = (1 - mine) * HALF + j
            t, v = split(transfer[s, :BS, :BS]), inflow[j, :BS]
            out[s * BS : (s + 1) * BS, 0] = offset[s] + (mm(t[0], v) + mm(t[1], v))

    pl.when(c == 0)(lambda: body(0))
    pl.when(c == 1)(lambda: body(1))


VMEM = pl.BlockSpec(memory_space=pltpu.VMEM)
SMEM = pl.BlockSpec(memory_space=pltpu.SMEM)
PARAMS = pltpu.CompilerParams(vmem_limit_bytes=20 << 20)


def hbm(*dims, dtype=F32):
    return jax.ShapeDtypeStruct(dims, dtype)


def vmem(*dims, dtype=F32):
    return pltpu.VMEM(dims, dtype)


def call(kernel, outs, args, scratch=()):
    scalar = [a.dtype == jnp.int32 for a in args]
    args = [a if one else pltpu.with_memory_space_constraint(a, pltpu.VMEM) for a, one in zip(args, scalar)]
    return pl.pallas_call(
        kernel,
        out_shape=outs,
        in_specs=[SMEM if one else VMEM for one in scalar],
        out_specs=jax.tree.map(lambda _: VMEM, outs, is_leaf=lambda o: not isinstance(o, tuple)),
        scratch_shapes=scratch,
        compiler_params=PARAMS,
    )(*args)


def local(inverses, couplings, rhs, previous, slot_layer):
    inv, rhs, prev = inverses[0, 0], rhs[0, 0], previous[0, 0]
    place = lax.axis_index("sweep").reshape(1).astype(jnp.int32)
    n_sweep, n_span = lax.axis_size("sweep"), lax.axis_size("span")
    swap = [(i, i ^ 1) for i in range(n_sweep)]
    wide = pltpu.VMEM((2, SECOND, 2 * LANE), F32)

    lower = lax.ppermute(prev, "span", [(i, (i + 1) % n_span) for i in range(n_span)])
    upper = lax.ppermute(prev, "span", [((i + 1) % n_span, i) for i in range(n_span)])
    down = lax.ppermute(prev, "sweep", [(i + 1, i) for i in range(n_sweep - 1)])

    anywhere = pl.BlockSpec(memory_space=pl.ANY)
    whole = [pltpu.with_memory_space_constraint(a, pltpu.HBM) for a in (slot_layer, inv, couplings, rhs, prev)]
    inv, last, near, transfer, send, partial = pl.pallas_call(
        local_kernel,
        out_shape=(
            vmem(NZ, BS, BS, dtype=BF16),
            vmem(NZ, BS, BS, dtype=BF16),
            vmem(NZ, BS, BS, dtype=BF16),
            vmem(NZ, ROWS, 2 * LANE),
            hbm(HALF, ROWS, 2 * LANE),
            vmem(NZ, BS, NRHS),
        ),
        in_specs=[SMEM] + [anywhere] * 5,
        out_specs=(VMEM,) * 6,
        scratch_shapes=[
            pltpu.SMEM((1, 1, NZ), jnp.int32),
            pltpu.VMEM((NZ, BS, BS), BF16),
            pltpu.VMEM((2, NZ, BS, BS), BF16),
            pltpu.VMEM((NZ, BS, NRHS), BF16),
            pltpu.VMEM((NZ, BS, NRHS), BF16),
            pltpu.SemaphoreType.DMA((9,)),
        ],
        name="local_kernel",
        compiler_params=PARAMS,
    )(place, *whole)
    sib = lax.ppermute(send, "sweep", swap)
    packed = call(product_kernel, vmem(HALF, PACKED, LANE, dtype=BF16), [place, transfer, sib], [wide])
    partial = pl.pallas_call(
        early_kernel,
        out_shape=vmem(NZ, BS, NRHS),
        in_specs=[anywhere] + [VMEM] * 4,
        input_output_aliases={2: 0},
        out_specs=VMEM,
        scratch_shapes=[pltpu.VMEM((NZ, BS, BS), BF16), pltpu.SemaphoreType.DMA(())],
        name="early_kernel",
        compiler_params=PARAMS,
    )(whole[2], *(pltpu.with_memory_space_constraint(a, pltpu.VMEM) for a in (near, partial, down, lower)))
    offset, send = call(
        offset_kernel,
        (vmem(NZ, BS, NRHS), vmem(HALF, ROWS, NRHS)),
        [place, inv, last, partial, upper],
    )
    offset_sib = lax.ppermute(send, "sweep", swap)
    send = call(
        pair_kernel, vmem(RUN, CHIP, LANE, dtype=BF16), [place, packed, transfer, sib, offset, offset_sib]
    )
    maps = lax.all_to_all(send, "sweep", 0, 0, axis_index_groups=RUNS)
    prefix, shifts, total = call(
        chain_kernel,
        (
            vmem(RUN - 1, 2, BS, BS, dtype=BF16),
            vmem(RUN - 1, BS, NRHS),
            vmem(AFFINE, LANE, dtype=BF16),
        ),
        [maps],
        [pltpu.VMEM((RUN, 2, SECOND, 2 * LANE), BF16), wide],
    )
    totals = lax.all_gather(total, "sweep", axis_index_groups=ACROSS)
    back = call(
        state_kernel,
        vmem(RUN, ROWS, NRHS, dtype=BF16),
        [place, totals, prefix, shifts],
        [pltpu.VMEM((BS, NRHS), F32), pltpu.VMEM((2, SECOND, 2 * LANE), BF16)],
    )
    inflow = lax.all_to_all(back, "sweep", 0, 0, axis_index_groups=RUNS)
    send = call(relay_kernel, vmem(HALF, ROWS, NRHS, dtype=BF16), [place, transfer, offset, inflow])
    half = call(half_kernel, vmem(HALF, BS, NRHS), [place, transfer, offset, sib, offset_sib, inflow])
    inflow = lax.ppermute(send, "sweep", swap)
    out = call(final_kernel, hbm(NZ * BS, 1, NRHS), [place, transfer, offset, half, inflow])
    return out.reshape(1, 1, NZ, BS, NRHS)


def solution(mesh):
    return jax.shard_map(
        local,
        mesh=mesh,
        in_specs=(
            P("sweep", "span", None, None, None),
            P(None, "sweep", "span", None, None, None),
            P("sweep", "span", None, None, None),
            P("sweep", "span", None, None, None),
            P("sweep", "span", None),
        ),
        out_specs=P("sweep", "span", None, None, None),
        check_vma=False,
    )
```
